32 devices in a mesh: inst: 4 (over x, core), lab: 8 (over z, y).
Axes of the slice: x: 2, y: 2, z: 4, core: 2. Of those that a mesh axis runs over, the one named last changes fastest.
Arguments:
- features: bfloat16 [2048, 768], P('inst'), may hold values from -6 to 6
- tile_rows: int32 [128], P(('inst', 'lab')), may hold values from 0 to 1, as said below
- tile_labels: int32 [128], P(('inst', 'lab')), may hold values from 0 to 3
- tile_values: bfloat16 [128, 256, 256], P(('inst', 'lab')), may hold values from 0 to 1
- cluster_ids: int32 [8192], P(('lab', 'inst')), may hold values from 0 to 1023, as said below
Outputs:
- label_embed: float32 [8192, 768], P(('lab', 'inst'))
- centroids: float32 [1024, 768], P(('inst', 'lab'))
The draws below stay inside these ranges and needn't reach their ends.
Inputs may be any that keep to these rules, and one draw needn't show every extreme that they name: Within each block of 4 entries the pairs (tile_rows, tile_labels) are distinct. Within each aligned block of 256 labels, at most 16 labels have clusters with the same value of cluster_ids // 32, and that many is reached in every block.
All inputs are finite; a program needn't handle non-finite values.
Results may differ from the reference program's by a relative error of at most 0.01.
Values may be sent and summed in bfloat16 or wider, within the bound.
A program may use at most 128 MiB of HBM per device.

```python
import jax
import jax.numpy as jnp
from jax import lax

D = 768
TILE = 256
INST_DEV = 512
LAB_DEV = 256
CL_OWN = 32
OWNERS = 32
RT = 2
LT = 4
NT_DEV = 4
TILES = 128
INSTANCES = 2048
CLUST = 1024
N_INST = 4
N_LAB = 8


def tile_pairs(key):
    keys = jax.random.split(jax.random.fold_in(key, 17), OWNERS)

    def pick(single):
        return jax.random.permutation(single, RT * LT)[:NT_DEV]
    picks = jax.vmap(pick)(keys).reshape(-1).astype(jnp.int32)
    return (picks // LT, picks % LT)


def draw_tile_rows(key, part):
    return tile_pairs(key)[0]


def draw_tile_labels(key, part):
    return tile_pairs(key)[1]


def draw_cluster_ids(key, part):
    keys = jax.random.split(jax.random.fold_in(key, 5), OWNERS)
    lowest = max(1, OWNERS // 16)

    def block(single):
        first, second, third, fourth = jax.random.split(single, 4)
        order = jax.random.permutation(first, OWNERS).astype(jnp.int32)
        doubled = jax.random.randint(second, (), lowest, OWNERS // 2 + 1)
        ranks = jnp.arange(LAB_DEV, dtype=jnp.int32) % OWNERS
        ranks = jnp.where(ranks >= OWNERS - doubled, ranks - (OWNERS - doubled), ranks)
        owner = order[ranks]
        inside = jax.random.randint(third, (LAB_DEV,), 0, CL_OWN)
        return jax.random.permutation(fourth, owner * CL_OWN + inside)
    return jax.vmap(block)(keys).reshape(-1).astype(jnp.int32)


def block_scale(own_key, dims, cuts, least, largest):
    def one(axis_at, blocks):
        steps = jax.random.uniform(jax.random.fold_in(jax.random.fold_in(own_key, 6), axis_at), (blocks,), jnp.float32, least / len(cuts), largest / len(cuts))
        return jnp.repeat(jnp.exp(steps), dims[axis_at] // blocks).reshape((-1,) + (1,) * (len(dims) - axis_at - 1))

    level = one(*cuts[0])
    for cut in cuts[1:]:
        level = level * one(*cut)
    return level


def normal_values(own_key, extent, width, reach, cuts=(), kind=jnp.bfloat16):
    level = block_scale(own_key, extent, cuts, -0.22, 0.18) if cuts else 1.0
    values = jax.random.normal(own_key, extent, jnp.float32) * width * level
    return jnp.minimum(jnp.maximum(values, -reach), reach).astype(kind)


def setup_inputs(seed: int = 0) -> dict:
    seeds = jax.random.split(jax.random.key(seed), 6)
    features = normal_values(seeds[0], (INSTANCES, D), 1.0, 6.0, ((0, 4),))
    tile_rows = draw_tile_rows(jax.random.fold_in(seeds[5], 71), 0)
    tile_labels = draw_tile_labels(jax.random.fold_in(seeds[5], 71), 0)
    tile_values = jnp.clip(1.0 * jax.random.uniform(seeds[3], (TILES, TILE, TILE), jnp.float32) ** block_scale(seeds[3], (TILES, TILE, TILE), ((0, 32),), -0.2, 0.2), 0.0, 1.0).astype(jnp.bfloat16)
    cluster_ids = draw_cluster_ids(jax.random.fold_in(seeds[5], 71), 0)
    return {"features": features, "tile_rows": tile_rows, "tile_labels": tile_labels, "tile_values": tile_values, "cluster_ids": cluster_ids}


def unit_rows(matrix):
    return matrix * lax.rsqrt(lax.optimization_barrier(jnp.sum(matrix * matrix, axis=-1, keepdims=True)) + 1e-06)

def reference(features, tile_rows, tile_labels, tile_values, cluster_ids):
    normed = unit_rows(features.astype(jnp.float32)).astype(jnp.bfloat16)
    row_tiles = INST_DEV // TILE
    lab_tiles = LAB_DEV * N_INST // TILE
    block_rows = LAB_DEV * N_INST
    shard_x = normed.reshape(N_INST, row_tiles, TILE, D)
    rows_all = tile_rows.reshape(N_INST, N_LAB, NT_DEV)
    labs_all = tile_labels.reshape(N_INST, N_LAB, NT_DEV)
    vals_all = tile_values.reshape(N_INST, N_LAB, NT_DEV, TILE, TILE)

    def shard_step(carry, pieces):
        xs, rr, cc, vv = pieces

        def one_block(parts):
            row_ids, lab_ids, values = parts
            picked = xs[row_ids].astype(jnp.float32)
            prod = jnp.einsum('nrl,nrd->nld', values.astype(jnp.float32), picked)
            seg = jax.ops.segment_sum(prod, lab_ids, num_segments=lab_tiles)
            return seg.reshape(block_rows, D).astype(jnp.bfloat16)
        partial_value = lax.map(one_block, (rr, cc, vv))
        return (carry + partial_value.astype(jnp.float32), None)
    start = jnp.zeros((N_LAB, block_rows, D), jnp.float32)
    summed, _ = lax.scan(shard_step, start, (shard_x, rows_all, labs_all, vals_all))
    label_embed = unit_rows(summed.reshape(N_LAB * block_rows, D))
    cluster_sums = jax.ops.segment_sum(label_embed, cluster_ids, num_segments=CLUST)
    return (label_embed, unit_rows(cluster_sums))
```

```python
import functools

import jax
import jax.numpy as jnp
from jax import lax
from jax.experimental import pallas as pl
from jax.experimental.pallas import tpu as pltpu
from jax.sharding import PartitionSpec as P

CL_OWN = 32
PAIR = 2
LAG = 3
MESH = pl.DeviceIdType.MESH


def unit_rows(matrix):
    return matrix * lax.rsqrt(jnp.sum(matrix * matrix, axis=-1, keepdims=True) + 1e-06)


def segments(tile):
    part = tile // 8
    tail = part // 2
    return [(q * part, part) for q in range(7)] + [(7 * part, tail), (7 * part + tail, tail)]


def blocks(tile):
    return [(0, tile // 2), (tile // 2, 3 * tile // 4), (3 * tile // 4, tile)]


def kernel(
    nx, ny, nz,
    rows_hbm, labs_hbm, ids_hbm, feat_hbm, val_hbm,
    emb_ref, cen_ref,
    rows_s, labs_s, feat, vals, xn, vt, csend, crecv, xsend, xrecv, total,
    eb, ids, picks0, picks1, picks2, acc,
    sa, ra, oa, sb, rb, ob, ya_s, ya_r, fa, xb_s, xb_r, fb, z_s, z_r,
    m_in, m_val, m_feat,
    s_core, r_core, s_x, r_x, s_zg, r_zg, s_cg, r_cg, s_fw, r_fw, s_ids, r_ids,
    s_sa, r_sa, s_sb, r_sb, s_ya, r_ya, s_xb, r_xb, s_za, r_za, s_zb, r_zb,
):
    inst = lax.axis_index("inst")
    lab = lax.axis_index("lab")
    x, c = inst // 2, inst % 2
    z, y = lab // ny, lab % ny
    other = 1 - c
    n_tiles, tile = val_hbm.shape[0], val_hbm.shape[1]
    width = feat_hbm.shape[1]
    half = width // 2
    row_tiles = feat_hbm.shape[0] // tile
    segs = segments(tile)
    cuts = blocks(tile)
    n_seg = len(segs)

    x_at = lambda d: (x + d) % nx
    y_at = lambda d: (y + d) % ny
    zq, zr = z // PAIR, z % PAIR
    nq = nz // PAIR
    zq_at = lambda d: (zq + d) % nq
    core_peer = (x * 2 + other, lab)
    x_peer = lambda d: (x_at(d) * 2 + c, lab)
    y_peer = lambda d: (inst, z * ny + y_at(d))
    z_peer = lambda d: (inst, (zq_at(d) * PAIR + zr) * ny + y)
    pair_peer = (inst, (zq * PAIR + (PAIR - 1 - zr)) * ny + y)
    peers = [core_peer]
    peers += [x_peer(d) for d in range(1, nx)]
    peers += [y_peer(d) for d in range(1, ny)]
    peers += [z_peer(d) for d in range(1, nq)]
    peers.append(pair_peer)

    barrier = pltpu.get_barrier_semaphore()
    for peer in peers:
        pl.semaphore_signal(barrier, inc=1, device_id=peer, device_id_type=MESH)

    loads = [
        pltpu.make_async_copy(rows_hbm, rows_s, m_in.at[0]),
        pltpu.make_async_copy(labs_hbm, labs_s, m_in.at[1]),
    ]
    val_loads = [
        pltpu.make_async_copy(val_hbm.at[n], vals.at[n], m_val.at[n]) for n in range(n_tiles)
    ]
    feat_loads = [
        pltpu.make_async_copy(
            feat_hbm.at[pl.ds(r * tile, tile)], feat.at[pl.ds(r * tile, tile)], m_feat.at[r]
        )
        for r in range(row_tiles)
    ]
    ids_load = pltpu.make_async_copy(ids_hbm, ids.at[0], m_in.at[2])
    for copy in [*loads, *val_loads, *feat_loads, ids_load]:
        copy.start()

    def remote(src, dst, send, recv, peer):
        return pltpu.make_async_remote_copy(
            src_ref=src, dst_ref=dst, send_sem=send, recv_sem=recv,
            device_id=peer, device_id_type=MESH,
        )

    sent = []

    def go(copy):
        copy.start()
        sent.append(copy)
        return copy

    vt[n_tiles] = jnp.zeros((tile, tile), jnp.bfloat16)
    with jax.named_scope("A_wval"):
        for n in range(n_tiles):
            val_loads[n].wait()
            vt[n] = vals[n].T
    with jax.named_scope("B_wfeat"):
        for r in range(row_tiles):
            feat_loads[r].wait()
            rows = pl.ds(r * tile, tile)
            xn[rows] = unit_rows(feat[rows].astype(jnp.float32)).astype(jnp.bfloat16)
    for copy in loads:
        copy.wait()

    def partial(label_tile, rows):
        pieces = []
        for r in range(row_tiles):
            at = jnp.int32(n_tiles)
            for n in range(n_tiles):
                hit = jnp.logical_and(rows_s[n] == r, labs_s[n] == label_tile)
                at = jnp.where(hit, n, at)
            pieces.append(vt[at, rows])
        lhs = jnp.concatenate(pieces, axis=1)
        return jnp.dot(lhs, xn[...], preferred_element_type=jnp.float32)

    mid = tile // 2
    halves = [(0, mid), (mid, tile)]

    def core_copies(xp, low, high):
        return {
            q: remote(
                csend.at[xp, pl.ds(first, size)], crecv.at[xp, pl.ds(first, size)],
                s_core.at[xp, q], r_core.at[xp, q], core_peer,
            )
            for q, (first, size) in enumerate(segs)
            if low <= first < high
        }

    id_copies = [
        remote(ids.at[0], ids.at[1], s_ids.at[0], r_ids.at[0], core_peer),
        remote(ids.at[0], ids.at[2], s_ids.at[1], r_ids.at[1], pair_peer),
        remote(ids.at[2], ids.at[3], s_ids.at[2], r_ids.at[2], core_peer),
    ]
    x_copies = {}
    met = False
    for d in [*range(1, nx), 0]:
        xp = x_at(d)
        arriving = {}
        for low, high in halves:
            rows = pl.ds(low, high - low)
            with jax.named_scope("D_part%d" % d):
                csend[xp, rows] = partial(xp * 2 + other, rows).astype(jnp.bfloat16)
            if not met:
                met = True
                with jax.named_scope("C_barrier"):
                    pl.semaphore_wait(barrier, len(peers))
                ids_load.wait()
                go(id_copies[0])
                go(id_copies[1])
            for q, copy in core_copies(xp, low, high).items():
                arriving[q] = go(copy)
        with jax.named_scope("E_own%d" % d):
            total[...] = partial(xp * 2 + c, pl.ds(0, tile))
        for q, (first, size) in enumerate(segs):
            rows = pl.ds(first, size)
            with jax.named_scope("F_w%d_%d" % (d, q)):
                arriving[q].wait_recv()
            mixed = total[rows] + crecv[xp, rows].astype(jnp.float32)
            if d:
                xsend[d - 1, rows] = mixed.astype(jnp.bfloat16)
                x_copies[d, q] = go(
                    remote(
                        xsend.at[d - 1, rows], xrecv.at[d - 1, rows],
                        s_x.at[d - 1, q], r_x.at[d - 1, q], x_peer(d),
                    )
                )
            else:
                total[rows] = mixed

    def mark(picks, low, high):
        near = jnp.concatenate([ids[s, :, low:high] for s in range(2 * PAIR)], axis=1)
        count = 2 * PAIR * (high - low)
        near = jnp.broadcast_to(near, (CL_OWN, count))
        step = lax.broadcasted_iota(jnp.int32, (CL_OWN, count), 0)
        row = 0
        for dz in range(nq):
            for dx in range(nx):
                for dy in range(ny):
                    owner = (x_at(dx) * 2 + c) * nz + zq_at(dz) * PAIR + zr
                    base = (owner * ny + y_at(dy)) * CL_OWN
                    hit = jnp.where(near == step + base, 1.0, 0.0)
                    picks[pl.ds(row, CL_OWN)] = hit.astype(jnp.bfloat16)
                    row += CL_OWN

    pair_rows, core_rows, passed = {}, {}, {}

    def fetch(q):
        rows = pl.ds(*segs[q])
        with jax.named_scope("I_fetch%d" % q):
            pair_rows[q].wait_recv()
        passed[q] = go(
            remote(eb.at[2, rows], eb.at[3, rows], s_fw.at[q], r_fw.at[q], core_peer)
        )

    def gathered(cut):
        for q, (first, _) in enumerate(segs):
            if cut[0] <= first < cut[1]:
                core_rows[q].wait_recv()
                passed[q].wait_recv()
        return eb[:, cut[0] : cut[1]].reshape(2 * PAIR * (cut[1] - cut[0]), width)

    for q, (first, size) in enumerate(segs):
        rows = pl.ds(first, size)
        value = total[rows]
        with jax.named_scope("H_wx%d" % q):
            for d in range(1, nx):
                x_copies[d, q].wait_recv()
        for d in range(1, nx):
            value += xrecv[d - 1, rows].astype(jnp.float32)
        value = unit_rows(value)
        emb_ref[rows] = value
        eb[0, rows] = value.astype(jnp.bfloat16)
        pair_rows[q] = go(
            remote(eb.at[0, rows], eb.at[2, rows], s_zg.at[q], r_zg.at[q], pair_peer)
        )
        core_rows[q] = go(
            remote(eb.at[0, rows], eb.at[1, rows], s_cg.at[q], r_cg.at[q], core_peer)
        )
        if q == 1:
            with jax.named_scope("G_ids2"):
                id_copies[1].wait_recv()
                go(id_copies[2])
        if q == LAG:
            with jax.named_scope("G_ids3"):
                id_copies[0].wait_recv()
                id_copies[2].wait_recv()
            with jax.named_scope("G_mark"):
                for picks, cut in zip((picks0, picks1, picks2), cuts):
                    mark(picks, *cut)
        if q >= LAG:
            fetch(q - LAG)
        if q == n_seg - 2:
            with jax.named_scope("J_block0"):
                acc[...] = jnp.dot(
                    picks0[...], gathered(cuts[0]), preferred_element_type=jnp.float32
                )

    fetch(n_seg - LAG)
    with jax.named_scope("J_block1"):
        acc[...] += jnp.dot(picks1[...], gathered(cuts[1]), preferred_element_type=jnp.float32)
    for q in range(n_seg - LAG + 1, n_seg):
        fetch(q)
    with jax.named_scope("J_wait2"):
        last = gathered(cuts[2])

    group = nx * ny * CL_OWN
    order = [*range(1, nq), 0]
    a1, b1, a2, b2, zs = {}, {}, {}, {}, []
    for dz in order:
        rows = pl.ds(dz * group, group)
        with jax.named_scope("J_block2_%d" % dz):
            value = acc[rows] + jnp.dot(picks2[rows], last, preferred_element_type=jnp.float32)
            value = value.reshape(nx, ny, CL_OWN, width)
            for d in range(1, nx):
                sa[dz, d - 1] = value[d, :, :, :half].astype(jnp.bfloat16)
                a1[dz, d] = go(
                    remote(
                        sa.at[dz, d - 1], ra.at[dz, d - 1],
                        s_sa.at[dz, d - 1], r_sa.at[dz, d - 1], x_peer(d),
                    )
                )
            for d in range(1, ny):
                sb[dz, d - 1] = value[:, d, :, half:].astype(jnp.bfloat16)
                b1[dz, d] = go(
                    remote(
                        sb.at[dz, d - 1], rb.at[dz, d - 1],
                        s_sb.at[dz, d - 1], r_sb.at[dz, d - 1], y_peer(d),
                    )
                )
            oa[dz] = value[0, :, :, :half]
            ob[dz] = value[:, 0, :, half:]

    for dz in order:
        with jax.named_scope("L_wxa%d" % dz):
            for d in range(1, nx):
                a1[dz, d].wait_recv()
        for k in range(ny - 1, -1, -1):
            mine = oa[dz, k]
            for d in range(1, nx):
                mine += ra[dz, d - 1, k].astype(jnp.float32)
            if k:
                ya_s[dz, k - 1] = mine.astype(jnp.bfloat16)
                a2[dz, k] = go(
                    remote(
                        ya_s.at[dz, k - 1], ya_r.at[dz, k - 1],
                        s_ya.at[dz, k - 1], r_ya.at[dz, k - 1], y_peer(k),
                    )
                )
            else:
                fa[dz] = mine
        with jax.named_scope("L_wyb%d" % dz):
            for d in range(1, ny):
                b1[dz, d].wait_recv()
        for k in range(nx - 1, -1, -1):
            mine = ob[dz, k]
            for d in range(1, ny):
                mine += rb[dz, d - 1, k].astype(jnp.float32)
            if k:
                xb_s[dz, k - 1] = mine.astype(jnp.bfloat16)
                b2[dz, k] = go(
                    remote(
                        xb_s.at[dz, k - 1], xb_r.at[dz, k - 1],
                        s_xb.at[dz, k - 1], r_xb.at[dz, k - 1], x_peer(k),
                    )
                )
            else:
                fb[dz] = mine

    own = []
    for dz in order:
        for side, got, arrived, ahead, count, s_z, r_z in (
            (0, a2, ya_r, fa, ny, s_za, r_za),
            (1, b2, xb_r, fb, nx, s_zb, r_zb),
        ):
            with jax.named_scope("M_w%d_%d" % (dz, side)):
                for k in range(1, count):
                    got[dz, k].wait_recv()
            mine = ahead[dz]
            for k in range(1, count):
                mine += arrived[dz, k - 1].astype(jnp.float32)
            if dz:
                z_s[side, dz - 1] = mine.astype(jnp.bfloat16)
                zs.append(
                    go(
                        remote(
                            z_s.at[side, dz - 1], z_r.at[side, dz - 1],
                            s_z.at[dz - 1], r_z.at[dz - 1], z_peer(dz),
                        )
                    )
                )
            else:
                own.append(mine)
    with jax.named_scope("N_wz"):
        for copy in zs:
            copy.wait_recv()
    with jax.named_scope("O_fin"):
        for side in range(2):
            for d in range(1, nq):
                own[side] += z_r[side, d - 1].astype(jnp.float32)
        cen_ref[...] = unit_rows(jnp.concatenate(own, axis=1))

    with jax.named_scope("P_wsend"):
        for copy in sent:
            copy.wait_send()


def write_out(emb, cen, emb_out, cen_out, sem):
    copies = [
        pltpu.make_async_copy(emb, emb_out, sem.at[0]),
        pltpu.make_async_copy(cen, cen_out, sem.at[1]),
    ]
    for copy in copies:
        copy.start()
    for copy in copies:
        copy.wait()


def shards(features, tile_rows, tile_labels, tile_values, cluster_ids):
    n_tiles, tile = tile_values.shape[:2]
    width = features.shape[1]
    labels = cluster_ids.shape[0]
    n_inst, n_lab = lax.axis_size("inst"), lax.axis_size("lab")
    nx = n_inst // 2
    ny = nx if n_lab % nx == 0 else 1
    nz = n_lab // ny
    assert labels == tile and nz % PAIR == 0
    nq = nz // PAIR
    half = width // 2
    bf, f32 = jnp.bfloat16, jnp.float32
    ox, oy, oq = max(nx - 1, 1), max(ny - 1, 1), max(nq - 1, 1)
    segs, cuts = len(segments(tile)), blocks(tile)
    dma = lambda *shape: [pltpu.SemaphoreType.DMA(shape)] * 2
    vmem = pl.BlockSpec(memory_space=pltpu.VMEM)
    hbm = pl.BlockSpec(memory_space=pl.ANY)
    sums = nq * nx * ny * CL_OWN
    emb, cen = pl.pallas_call(
        functools.partial(kernel, nx, ny, nz),
        out_shape=(
            pltpu.VMEM((labels, width), f32),
            pltpu.VMEM((CL_OWN, width), f32),
        ),
        in_specs=[hbm] * 5,
        out_specs=(vmem, vmem),
        scratch_shapes=[
            pltpu.SMEM((n_tiles,), jnp.int32),
            pltpu.SMEM((n_tiles,), jnp.int32),
            pltpu.VMEM(features.shape, bf),
            pltpu.VMEM(tile_values.shape, bf),
            pltpu.VMEM(features.shape, bf),
            pltpu.VMEM((n_tiles + 1, tile, tile), bf),
            pltpu.VMEM((nx, tile, width), bf),
            pltpu.VMEM((nx, tile, width), bf),
            pltpu.VMEM((ox, tile, width), bf),
            pltpu.VMEM((ox, tile, width), bf),
            pltpu.VMEM((tile, width), f32),
            pltpu.VMEM((2 * PAIR, tile, width), bf),
            pltpu.VMEM((2 * PAIR, 1, tile), jnp.int32),
            *[pltpu.VMEM((sums, 2 * PAIR * (high - low)), bf) for low, high in cuts],
            pltpu.VMEM((sums, width), f32),
            pltpu.VMEM((nq, ox, ny, CL_OWN, half), bf),
            pltpu.VMEM((nq, ox, ny, CL_OWN, half), bf),
            pltpu.VMEM((nq, ny, CL_OWN, half), f32),
            pltpu.VMEM((nq, oy, nx, CL_OWN, half), bf),
            pltpu.VMEM((nq, oy, nx, CL_OWN, half), bf),
            pltpu.VMEM((nq, nx, CL_OWN, half), f32),
            pltpu.VMEM((nq, oy, CL_OWN, half), bf),
            pltpu.VMEM((nq, oy, CL_OWN, half), bf),
            pltpu.VMEM((nq, CL_OWN, half), f32),
            pltpu.VMEM((nq, ox, CL_OWN, half), bf),
            pltpu.VMEM((nq, ox, CL_OWN, half), bf),
            pltpu.VMEM((nq, CL_OWN, half), f32),
            pltpu.VMEM((2, oq, CL_OWN, half), bf),
            pltpu.VMEM((2, oq, CL_OWN, half), bf),
            pltpu.SemaphoreType.DMA((3,)),
            pltpu.SemaphoreType.DMA((n_tiles,)),
            pltpu.SemaphoreType.DMA((features.shape[0] // tile,)),
            *dma(nx, segs),
            *dma(ox, segs),
            *dma(segs),
            *dma(segs),
            *dma(segs),
            *dma(3),
            *dma(nq, ox),
            *dma(nq, oy),
            *dma(nq, oy),
            *dma(nq, ox),
            *dma(oq),
            *dma(oq),
        ],
        compiler_params=pltpu.CompilerParams(
            collective_id=0, has_side_effects=True, vmem_limit_bytes=60 * 1024 * 1024
        ),
        name="pifa_step",
    )(tile_rows, tile_labels, cluster_ids.reshape(1, labels), features, tile_values)
    return pl.pallas_call(
        write_out,
        out_shape=(
            jax.ShapeDtypeStruct((labels, width), f32),
            jax.ShapeDtypeStruct((CL_OWN, width), f32),
        ),
        in_specs=[vmem, vmem],
        out_specs=(hbm, hbm),
        scratch_shapes=[pltpu.SemaphoreType.DMA((2,))],
        name="write_out",
    )(
        pltpu.with_memory_space_constraint(emb, pltpu.VMEM),
        pltpu.with_memory_space_constraint(cen, pltpu.VMEM),
    )


def solution(mesh):
    return jax.shard_map(
        shards,
        mesh=mesh,
        in_specs=(
            P("inst", None),
            P(("inst", "lab")),
            P(("inst", "lab")),
            P(("inst", "lab"), None, None),
            P(("lab", "inst")),
        ),
        out_specs=(P(("lab", "inst"), None), P(("inst", "lab"), None)),
        check_vma=False,
    )
```

```python
import functools

import jax
import jax.numpy as jnp
from jax import lax
from jax.experimental import pallas as pl
from jax.experimental.pallas import tpu as pltpu
from jax.sharding import PartitionSpec as P

CL_OWN = 32
PAIR = 2
LAG = 4
DIRECT = 1
SPLIT = 2
MESH = pl.DeviceIdType.MESH


def unit_rows(matrix):
    return matrix * lax.rsqrt(jnp.sum(matrix * matrix, axis=-1, keepdims=True) + 1e-06)


def segments(tile):
    part = tile // 8
    tail = part // 2
    return [(q * part, part) for q in range(7)] + [(7 * part, tail), (7 * part + tail, tail)]


def blocks(tile):
    return [(0, tile // 2), (tile // 2, 3 * tile // 4), (3 * tile // 4, tile)]


def kernel(
    nx, ny, nz,
    rows_hbm, labs_hbm, ids_hbm, feat_hbm, val_hbm,
    emb_ref, cen_ref,
    rows_s, labs_s, feat, vals, xn, vt, csend, crecv, xsend, xrecv, total,
    eb, ids, picks0, picks1, picks2, acc,
    sa, ra, oa, sb, rb, ob, ya_s, ya_r, fa, xb_s, xb_r, fb, z_s, z_r,
    m_in, m_val, m_feat,
    s_core, r_core, s_x, r_x, s_zg, r_zg, s_cg, r_cg, s_fw, r_fw, s_ids, r_ids,
    s_sa, r_sa, s_sb, r_sb, s_ya, r_ya, s_xb, r_xb, s_za, r_za, s_zb, r_zb,
):
    inst = lax.axis_index("inst")
    lab = lax.axis_index("lab")
    x, c = inst // 2, inst % 2
    z, y = lab // ny, lab % ny
    other = 1 - c
    n_tiles, tile = val_hbm.shape[0], val_hbm.shape[1]
    width = feat_hbm.shape[1]
    half = width // 2
    row_tiles = feat_hbm.shape[0] // tile
    segs = segments(tile)
    cuts = blocks(tile)
    n_seg = len(segs)
    part = CL_OWN // SPLIT

    x_at = lambda d: (x + d) % nx
    y_at = lambda d: (y + d) % ny
    zq, zr = z // PAIR, z % PAIR
    nq = nz // PAIR
    zq_at = lambda d: (zq + d) % nq
    core_peer = (x * 2 + other, lab)
    x_peer = lambda d: (x_at(d) * 2 + c, lab)
    y_peer = lambda d: (inst, z * ny + y_at(d))
    z_peer = lambda d: (inst, (zq_at(d) * PAIR + zr) * ny + y)
    pair_peer = (inst, (zq * PAIR + (PAIR - 1 - zr)) * ny + y)
    peers = [core_peer]
    peers += [x_peer(d) for d in range(1, nx)]
    peers += [y_peer(d) for d in range(1, ny)]
    peers += [z_peer(d) for d in range(1, nq)]
    diag_peer = (x * 2 + other, pair_peer[1])
    peers += [diag_peer, pair_peer]

    barrier = pltpu.get_barrier_semaphore()
    for peer in peers:
        pl.semaphore_signal(barrier, inc=1, device_id=peer, device_id_type=MESH)

    loads = [
        pltpu.make_async_copy(rows_hbm, rows_s, m_in.at[0]),
        pltpu.make_async_copy(labs_hbm, labs_s, m_in.at[1]),
    ]
    val_loads = [
        pltpu.make_async_copy(val_hbm.at[n], vals.at[n], m_val.at[n]) for n in range(n_tiles)
    ]
    feat_loads = [
        pltpu.make_async_copy(
            feat_hbm.at[pl.ds(r * tile, tile)], feat.at[pl.ds(r * tile, tile)], m_feat.at[r]
        )
        for r in range(row_tiles)
    ]
    ids_load = pltpu.make_async_copy(ids_hbm, ids.at[0], m_in.at[2])
    for copy in [*loads, *val_loads, *feat_loads, ids_load]:
        copy.start()

    def remote(src, dst, send, recv, peer):
        return pltpu.make_async_remote_copy(
            src_ref=src, dst_ref=dst, send_sem=send, recv_sem=recv,
            device_id=peer, device_id_type=MESH,
        )

    sent = []

    def go(copy):
        copy.start()
        sent.append(copy)
        return copy

    vt[n_tiles] = jnp.zeros((tile, tile), jnp.bfloat16)
    with jax.named_scope("A_wval"):
        for n in range(n_tiles):
            val_loads[n].wait()
            vt[n] = vals[n].T
    with jax.named_scope("B_wfeat"):
        for r in range(row_tiles):
            feat_loads[r].wait()
            rows = pl.ds(r * tile, tile)
            xn[rows] = unit_rows(feat[rows].astype(jnp.float32)).astype(jnp.bfloat16)
    for copy in loads:
        copy.wait()

    def partial(label_tile, rows):
        pieces = []
        for r in range(row_tiles):
            at = jnp.int32(n_tiles)
            for n in range(n_tiles):
                hit = jnp.logical_and(rows_s[n] == r, labs_s[n] == label_tile)
                at = jnp.where(hit, n, at)
            pieces.append(vt[at, rows])
        lhs = jnp.concatenate(pieces, axis=1)
        return jnp.dot(lhs, xn[...], preferred_element_type=jnp.float32)

    mid = tile // 2
    halves = [(0, mid), (mid, tile)]

    def core_copies(xp, low, high):
        return {
            q: remote(
                csend.at[xp, pl.ds(first, size)], crecv.at[xp, pl.ds(first, size)],
                s_core.at[xp, q], r_core.at[xp, q], core_peer,
            )
            for q, (first, size) in enumerate(segs)
            if low <= first < high
        }

    id_copies = [
        remote(ids.at[0], ids.at[1], s_ids.at[0], r_ids.at[0], core_peer),
        remote(ids.at[0], ids.at[2], s_ids.at[1], r_ids.at[1], pair_peer),
        remote(ids.at[2], ids.at[3], s_ids.at[2], r_ids.at[2], core_peer),
    ]
    x_copies = {}
    met = False
    for d in [*range(1, nx), 0]:
        xp = x_at(d)
        arriving = {}
        for low, high in halves:
            rows = pl.ds(low, high - low)
            with jax.named_scope("D_part%d" % d):
                csend[xp, rows] = partial(xp * 2 + other, rows).astype(jnp.bfloat16)
            if not met:
                met = True
                with jax.named_scope("C_barrier"):
                    pl.semaphore_wait(barrier, len(peers))
                ids_load.wait()
                go(id_copies[0])
                go(id_copies[1])
            for q, copy in core_copies(xp, low, high).items():
                arriving[q] = go(copy)
        with jax.named_scope("E_own%d" % d):
            total[...] = partial(xp * 2 + c, pl.ds(0, tile))
        for q, (first, size) in enumerate(segs):
            rows = pl.ds(first, size)
            with jax.named_scope("F_w%d_%d" % (d, q)):
                arriving[q].wait_recv()
            mixed = total[rows] + crecv[xp, rows].astype(jnp.float32)
            if d:
                xsend[d - 1, rows] = mixed.astype(jnp.bfloat16)
                x_copies[d, q] = go(
                    remote(
                        xsend.at[d - 1, rows], xrecv.at[d - 1, rows],
                        s_x.at[d - 1, q], r_x.at[d - 1, q], x_peer(d),
                    )
                )
            else:
                total[rows] = mixed

    def mark(picks, low, high):
        near = jnp.concatenate([ids[s, :, low:high] for s in range(2 * PAIR)], axis=1)
        count = 2 * PAIR * (high - low)
        near = jnp.broadcast_to(near, (part, count))
        step = lax.broadcasted_iota(jnp.int32, (part, count), 0)
        row = 0
        for dz in range(nq):
            for g in range(SPLIT):
                for dx in range(nx):
                    for dy in range(ny):
                        owner = (x_at(dx) * 2 + c) * nz + zq_at(dz) * PAIR + zr
                        base = (owner * ny + y_at(dy)) * CL_OWN + g * part
                        hit = jnp.where(near == step + base, 1.0, 0.0)
                        picks[pl.ds(row, part)] = hit.astype(jnp.bfloat16)
                        row += part

    pair_rows, core_rows, passed = {}, {}, {}

    def fetch(q):
        rows = pl.ds(*segs[q])
        if q >= n_seg - DIRECT:
            return
        with jax.named_scope("I_fetch%d" % q):
            pair_rows[q].wait_recv()
        passed[q] = go(
            remote(eb.at[2, rows], eb.at[3, rows], s_fw.at[q], r_fw.at[q], core_peer)
        )

    def gathered(cut):
        for q, (first, _) in enumerate(segs):
            if cut[0] <= first < cut[1]:
                if q >= n_seg - DIRECT:
                    pair_rows[q].wait_recv()
                core_rows[q].wait_recv()
                passed[q].wait_recv()
        return eb[:, cut[0] : cut[1]].reshape(2 * PAIR * (cut[1] - cut[0]), width)

    for q, (first, size) in enumerate(segs):
        rows = pl.ds(first, size)
        value = total[rows]
        with jax.named_scope("H_wx%d" % q):
            for d in range(1, nx):
                x_copies[d, q].wait_recv()
        for d in range(1, nx):
            value += xrecv[d - 1, rows].astype(jnp.float32)
        value = unit_rows(value)
        emb_ref[rows] = value
        eb[0, rows] = value.astype(jnp.bfloat16)
        pair_rows[q] = go(
            remote(eb.at[0, rows], eb.at[2, rows], s_zg.at[q], r_zg.at[q], pair_peer)
        )
        if q >= n_seg - DIRECT:
            passed[q] = go(
                remote(eb.at[0, rows], eb.at[3, rows], s_fw.at[q], r_fw.at[q], diag_peer)
            )
        core_rows[q] = go(
            remote(eb.at[0, rows], eb.at[1, rows], s_cg.at[q], r_cg.at[q], core_peer)
        )
        if q == 1:
            with jax.named_scope("G_ids2"):
                id_copies[1].wait_recv()
                go(id_copies[2])
        if q == LAG:
            with jax.named_scope("G_ids3"):
                id_copies[0].wait_recv()
                id_copies[2].wait_recv()
            with jax.named_scope("G_mark"):
                for picks, cut in zip((picks0, picks1, picks2), cuts):
                    mark(picks, *cut)
        if q >= LAG:
            fetch(q - LAG)

    for q in range(n_seg - LAG, n_seg):
        if q == n_seg - 2:
            with jax.named_scope("J_block0"):
                acc[...] = jnp.dot(
                    picks0[...], gathered(cuts[0]), preferred_element_type=jnp.float32
                )
        fetch(q)
    with jax.named_scope("J_block1"):
        acc[...] += jnp.dot(picks1[...], gathered(cuts[1]), preferred_element_type=jnp.float32)
    with jax.named_scope("J_wait2"):
        last = gathered(cuts[2])

    group = nx * ny * CL_OWN
    far = [(dz, g) for dz in range(1, nq) for g in range(SPLIT)]
    home = [(0, g) for g in range(SPLIT)]
    a1, b1, a2, b2, zs = {}, {}, {}, {}, []

    def local(dz):
        rows = pl.ds(dz * group, group)
        value = acc[rows] + jnp.dot(picks2[rows], last, preferred_element_type=jnp.float32)
        value = value.reshape(SPLIT, nx, ny, part, width)
        for g in range(SPLIT):
            at = dz * SPLIT + g
            for d in range(1, nx):
                sa[at, d - 1] = value[g, d, :, :, :half].astype(jnp.bfloat16)
            for d in range(1, ny):
                sb[at, d - 1] = value[g, :, d, :, half:].astype(jnp.bfloat16)
            oa[at] = value[g, 0, :, :, :half]
            ob[at] = value[g, :, 0, :, half:]

    def first(dz, g):
        at = dz * SPLIT + g
        for d in range(1, nx):
            a1[dz, g, d] = go(
                remote(
                    sa.at[at, d - 1], ra.at[at, d - 1],
                    s_sa.at[at, d - 1], r_sa.at[at, d - 1], x_peer(d),
                )
            )
        for d in range(1, ny):
            b1[dz, g, d] = go(
                remote(
                    sb.at[at, d - 1], rb.at[at, d - 1],
                    s_sb.at[at, d - 1], r_sb.at[at, d - 1], y_peer(d),
                )
            )

    def second(dz, g):
        at = dz * SPLIT + g
        with jax.named_scope("L_wa%d%d" % (dz, g)):
            for d in range(1, nx):
                a1[dz, g, d].wait_recv()
        for k in range(ny - 1, -1, -1):
            mine = oa[at, k]
            for d in range(1, nx):
                mine += ra[at, d - 1, k].astype(jnp.float32)
            if k:
                ya_s[at, k - 1] = mine.astype(jnp.bfloat16)
                a2[dz, g, k] = go(
                    remote(
                        ya_s.at[at, k - 1], ya_r.at[at, k - 1],
                        s_ya.at[at, k - 1], r_ya.at[at, k - 1], y_peer(k),
                    )
                )
            else:
                fa[at] = mine
        with jax.named_scope("L_wb%d%d" % (dz, g)):
            for d in range(1, ny):
                b1[dz, g, d].wait_recv()
        for k in range(nx - 1, -1, -1):
            mine = ob[at, k]
            for d in range(1, ny):
                mine += rb[at, d - 1, k].astype(jnp.float32)
            if k:
                xb_s[at, k - 1] = mine.astype(jnp.bfloat16)
                b2[dz, g, k] = go(
                    remote(
                        xb_s.at[at, k - 1], xb_r.at[at, k - 1],
                        s_xb.at[at, k - 1], r_xb.at[at, k - 1], x_peer(k),
                    )
                )
            else:
                fb[at] = mine

    def third(dz, g):
        at = dz * SPLIT + g
        done = []
        for side, got, arrived, ahead, count, s_z, r_z in (
            (0, a2, ya_r, fa, ny, s_za, r_za),
            (1, b2, xb_r, fb, nx, s_zb, r_zb),
        ):
            with jax.named_scope("M_w%d%d_%d" % (dz, g, side)):
                for k in range(1, count):
                    got[dz, g, k].wait_recv()
            mine = ahead[at]
            for k in range(1, count):
                mine += arrived[at, k - 1].astype(jnp.float32)
            if dz:
                to = at - SPLIT
                z_s[side, to] = mine.astype(jnp.bfloat16)
                copy = remote(
                    z_s.at[side, to], z_r.at[side, to],
                    s_z.at[to], r_z.at[to], z_peer(dz),
                )
                zs.append(go(copy))
            done.append(mine)
        return done

    for dz in range(1, nq):
        with jax.named_scope("J_block2_%d" % dz):
            local(dz)
            for g in range(SPLIT):
                first(dz, g)
    with jax.named_scope("J_block2_0"):
        local(0)
    for piece in far:
        second(*piece)
    for piece in home:
        first(*piece)
    for piece in far:
        third(*piece)
    for piece in home:
        second(*piece)
    own = [third(*piece) for piece in home]
    with jax.named_scope("N_wz"):
        for copy in zs:
            copy.wait_recv()
    with jax.named_scope("O_fin"):
        for g in range(SPLIT):
            for side in range(2):
                for d in range(1, nq):
                    own[g][side] += z_r[side, (d - 1) * SPLIT + g].astype(jnp.float32)
            cen_ref[pl.ds(g * part, part)] = unit_rows(jnp.concatenate(own[g], axis=1))

    with jax.named_scope("P_wsend"):
        for copy in sent:
            copy.wait_send()


def write_out(emb, cen, emb_out, cen_out, sem):
    copies = [
        pltpu.make_async_copy(emb, emb_out, sem.at[0]),
        pltpu.make_async_copy(cen, cen_out, sem.at[1]),
    ]
    for copy in copies:
        copy.start()
    for copy in copies:
        copy.wait()


def shards(features, tile_rows, tile_labels, tile_values, cluster_ids):
    n_tiles, tile = tile_values.shape[:2]
    width = features.shape[1]
    labels = cluster_ids.shape[0]
    n_inst, n_lab = lax.axis_size("inst"), lax.axis_size("lab")
    nx = n_inst // 2
    ny = nx if n_lab % nx == 0 else 1
    nz = n_lab // ny
    assert labels == tile and nz % PAIR == 0
    nq = nz // PAIR
    half = width // 2
    bf, f32 = jnp.bfloat16, jnp.float32
    ox, oy, oq = max(nx - 1, 1), max(ny - 1, 1), max(nq - 1, 1)
    segs, cuts = len(segments(tile)), blocks(tile)
    dma = lambda *shape: [pltpu.SemaphoreType.DMA(shape)] * 2
    vmem = pl.BlockSpec(memory_space=pltpu.VMEM)
    hbm = pl.BlockSpec(memory_space=pl.ANY)
    part = CL_OWN // SPLIT
    sums = nq * nx * ny * CL_OWN
    emb, cen = pl.pallas_call(
        functools.partial(kernel, nx, ny, nz),
        out_shape=(
            pltpu.VMEM((labels, width), f32),
            pltpu.VMEM((CL_OWN, width), f32),
        ),
        in_specs=[hbm] * 5,
        out_specs=(vmem, vmem),
        scratch_shapes=[
            pltpu.SMEM((n_tiles,), jnp.int32),
            pltpu.SMEM((n_tiles,), jnp.int32),
            pltpu.VMEM(features.shape, bf),
            pltpu.VMEM(tile_values.shape, bf),
            pltpu.VMEM(features.shape, bf),
            pltpu.VMEM((n_tiles + 1, tile, tile), bf),
            pltpu.VMEM((nx, tile, width), bf),
            pltpu.VMEM((nx, tile, width), bf),
            pltpu.VMEM((ox, tile, width), bf),
            pltpu.VMEM((ox, tile, width), bf),
            pltpu.VMEM((tile, width), f32),
            pltpu.VMEM((2 * PAIR, tile, width), bf),
            pltpu.VMEM((2 * PAIR, 1, tile), jnp.int32),
            *[pltpu.VMEM((sums, 2 * PAIR * (high - low)), bf) for low, high in cuts],
            pltpu.VMEM((sums, width), f32),
            pltpu.VMEM((nq * SPLIT, ox, ny, part, half), bf),
            pltpu.VMEM((nq * SPLIT, ox, ny, part, half), bf),
            pltpu.VMEM((nq * SPLIT, ny, part, half), f32),
            pltpu.VMEM((nq * SPLIT, oy, nx, part, half), bf),
            pltpu.VMEM((nq * SPLIT, oy, nx, part, half), bf),
            pltpu.VMEM((nq * SPLIT, nx, part, half), f32),
            pltpu.VMEM((nq * SPLIT, oy, part, half), bf),
            pltpu.VMEM((nq * SPLIT, oy, part, half), bf),
            pltpu.VMEM((nq * SPLIT, part, half), f32),
            pltpu.VMEM((nq * SPLIT, ox, part, half), bf),
            pltpu.VMEM((nq * SPLIT, ox, part, half), bf),
            pltpu.VMEM((nq * SPLIT, part, half), f32),
            pltpu.VMEM((2, oq * SPLIT, part, half), bf),
            pltpu.VMEM((2, oq * SPLIT, part, half), bf),
            pltpu.SemaphoreType.DMA((3,)),
            pltpu.SemaphoreType.DMA((n_tiles,)),
            pltpu.SemaphoreType.DMA((features.shape[0] // tile,)),
            *dma(nx, segs),
            *dma(ox, segs),
            *dma(segs),
            *dma(segs),
            *dma(segs),
            *dma(3),
            *dma(nq * SPLIT, ox),
            *dma(nq * SPLIT, oy),
            *dma(nq * SPLIT, oy),
            *dma(nq * SPLIT, ox),
            *dma(oq * SPLIT),
            *dma(oq * SPLIT),
        ],
        compiler_params=pltpu.CompilerParams(
            collective_id=0, has_side_effects=True, vmem_limit_bytes=60 * 1024 * 1024
        ),
        name="pifa_step",
    )(tile_rows, tile_labels, cluster_ids.reshape(1, labels), features, tile_values)
    return pl.pallas_call(
        write_out,
        out_shape=(
            jax.ShapeDtypeStruct((labels, width), f32),
            jax.ShapeDtypeStruct((CL_OWN, width), f32),
        ),
        in_specs=[vmem, vmem],
        out_specs=(hbm, hbm),
        scratch_shapes=[pltpu.SemaphoreType.DMA((2,))],
        name="write_out",
    )(
        pltpu.with_memory_space_constraint(emb, pltpu.VMEM),
        pltpu.with_memory_space_constraint(cen, pltpu.VMEM),
    )


def solution(mesh):
    return jax.shard_map(
        shards,
        mesh=mesh,
        in_specs=(
            P("inst", None),
            P(("inst", "lab")),
            P(("inst", "lab")),
            P(("inst", "lab"), None, None),
            P(("lab", "inst")),
        ),
        out_specs=(P(("lab", "inst"), None), P(("inst", "lab"), None)),
        check_vma=False,
    )
```
